32 devices in a mesh: slab: 8 (over z, x), grp: 4 (over y, core).
Axes of the slice: x: 2, y: 2, z: 4, core: 2. Of those that a mesh axis runs over, the one named last changes fastest.
Arguments:
- iterate: float32 [3072, 256], P(('slab', 'grp')), may hold values from -6 to 6
- residual: float32 [3072, 256], P(('slab', 'grp')), may hold values from -6 to 6
- direction: float32 [3072, 256], P(('slab', 'grp')), may hold values from -6 to 6
- prior_rho: float32 [256], replicated, may hold values from 1536 to 6144
- diag_blocks: float32 [3072, 384], P(('slab', 'grp')), as said below
- lower_coupling: float32 [3072, 128], P(('slab', 'grp')), may hold values from -0.125 to 0.125
- upper_coupling: float32 [3072, 128], P(('slab', 'grp')), may hold values from -0.125 to 0.125
- interface: int32 [8, 128], P('slab'), may hold values from 0 to 383, as said below
- jacobi_inverse: float32 [3072, 96], P(('slab', 'grp'))
- slab_inverse: float32 [3072, 384], P(('slab', 'grp'))
- lower_factor: float32 [3072, 128], P(('slab', 'grp')), may hold values from -0.875 to 0.875
- upper_factor: float32 [3072, 128], P(('slab', 'grp')), may hold values from -0.5 to 0.5
Outputs:
- new_iterate: float32 [3072, 256], P(('slab', 'grp'))
- new_residual: float32 [3072, 256], P(('slab', 'grp'))
- new_direction: float32 [3072, 256], P(('slab', 'grp'))
- new_rho: float32 [256], replicated
The draws below stay inside these ranges and needn't reach their ends.
Inputs may be any that keep to these rules, and one draw needn't show every extreme that they name: `interface`: row k lists 128 distinct dof numbers of slab k. `diag_blocks`: each diagonal block is a positive diagonal plus a skew-symmetric part.
All inputs are finite; a program needn't handle non-finite values.
Results may differ from the reference program's by a relative error of at most 0.0003.
Values sent between devices are 32-bit elements; how exact they have to be, the bound alone decides.
A program may use at most 64 MiB of HBM per device.

```python
import math
import jax
import jax.numpy as jnp
from jax import lax

B = 384
IF = 128
R = 256
NSLAB = 8
GB = 96
ROWS = 3072
N_GRP = 4


def draw_diag_blocks(key, part):
    first, second = jax.random.split(jax.random.fold_in(key, 11))
    source = jax.random.normal(first, (NSLAB, B, B), jnp.float32) / B ** 0.5
    scales = jax.random.uniform(second, (NSLAB, B), jnp.float32, 1.0, 3.0)
    blocks = source - jnp.swapaxes(source, 1, 2) + scales[:, :, None] * jnp.eye(B, dtype=jnp.float32)[None]
    return blocks.reshape(NSLAB * B, B)


def draw_interface(key, part):
    keys = jax.random.split(jax.random.fold_in(key, 12), NSLAB)
    chosen = jax.vmap(lambda single: jax.random.permutation(single, B)[:IF])(keys)
    return chosen.astype(jnp.int32)


def draw_jacobi_inverse(key, part):
    noise = jax.random.normal(jax.random.fold_in(key, 13), (NSLAB * B, GB), jnp.float32) * (0.5 / GB ** 0.5)
    rowid = jnp.arange(NSLAB * B, dtype=jnp.int32)[:, None] % GB
    colid = jnp.arange(GB, dtype=jnp.int32)[None, :]
    return noise + 0.5 * (rowid == colid).astype(jnp.float32)


def draw_slab_inverse(key, part):
    noise = jax.random.normal(jax.random.fold_in(key, 14), (NSLAB * B, B), jnp.float32) * (0.3 / B ** 0.5)
    rowid = jnp.arange(NSLAB * B, dtype=jnp.int32)[:, None] % B
    colid = jnp.arange(B, dtype=jnp.int32)[None, :]
    return noise + 0.5 * (rowid == colid).astype(jnp.float32)


def steps_of(stream_key, extent, cuts, smallest, high):
    factor_of = 1.0
    for position, parts in cuts:
        draws = jax.random.uniform(jax.random.fold_in(jax.random.fold_in(stream_key, 6), position), (parts,), jnp.float32, smallest / len(cuts), high / len(cuts))
        factor_of = factor_of * jnp.repeat(jnp.exp(draws), extent[position] // parts).reshape((-1,) + (1,) * (len(extent) - 1 - position))
    return factor_of


def gaussian(stream_key, extent, spread, limit, cuts=(), kind=jnp.bfloat16):
    array = spread * jax.random.normal(stream_key, extent, jnp.float32)
    if cuts:
        array = array * steps_of(stream_key, extent, cuts, -0.22, 0.18)
    return jnp.clip(array, -limit, limit).astype(kind)


def setup_inputs(seed: int = 0) -> dict:
    arg_keys = jax.random.split(jax.random.key(seed), 13)
    iterate = gaussian(arg_keys[0], (ROWS, R), 1.0, 6.0, ((0, 32),), jnp.float32)
    residual = gaussian(arg_keys[1], (ROWS, R), 1.0, 6.0, ((0, 32),), jnp.float32)
    direction = gaussian(arg_keys[2], (ROWS, R), 1.0, 6.0, ((0, 32),), jnp.float32)
    prior_rho = jnp.clip(jnp.exp(jax.random.uniform(arg_keys[3], (R,), jnp.float32, math.log(1536.0), math.log(6144.0))), 1536.0, 6144.0)
    diag_blocks = draw_diag_blocks(jax.random.fold_in(arg_keys[12], 71), 0)
    lower_coupling = gaussian(arg_keys[5], (ROWS, IF), (16 * IF) ** -0.5, 0.125, ((0, 32),), jnp.float32)
    upper_coupling = gaussian(arg_keys[6], (ROWS, IF), (16 * IF) ** -0.5, 0.125, ((0, 32),), jnp.float32)
    interface = draw_interface(jax.random.fold_in(arg_keys[12], 71), 0)
    jacobi_inverse = draw_jacobi_inverse(jax.random.fold_in(arg_keys[12], 71), 0)
    slab_inverse = draw_slab_inverse(jax.random.fold_in(arg_keys[12], 71), 0)
    lower_factor = gaussian(arg_keys[10], (ROWS, IF), (IF * 13 // 36) ** -0.5, 0.875, ((0, 32),), jnp.float32)
    upper_factor = gaussian(arg_keys[11], (ROWS, IF), (IF * 17 // 16) ** -0.5, 0.5, ((0, 32),), jnp.float32)
    return {"iterate": iterate, "residual": residual, "direction": direction, "prior_rho": prior_rho, "diag_blocks": diag_blocks, "lower_coupling": lower_coupling, "upper_coupling": upper_coupling, "interface": interface, "jacobi_inverse": jacobi_inverse, "slab_inverse": slab_inverse, "lower_factor": lower_factor, "upper_factor": upper_factor}


def pick_rows(field, interface):
    return jax.vmap(lambda block, index: block[index])(field, interface)


def slab_apply(matrix, field):
    return jnp.einsum("kij,kjr->kir", matrix, field, precision=lax.Precision.HIGHEST)


def operate(field, diag_blocks, lower_coupling, upper_coupling, interface):
    faces = pick_rows(field, interface)
    zero_face = jnp.zeros_like(faces[:1])
    below = jnp.concatenate([zero_face, faces[:-1]], axis=0)
    above = jnp.concatenate([faces[1:], zero_face], axis=0)
    return slab_apply(diag_blocks, field) + slab_apply(lower_coupling, below) + slab_apply(upper_coupling, above)


def affine_step(carry, inputs):
    transfer, offset = inputs
    value = offset + jnp.dot(transfer, carry, precision=lax.Precision.HIGHEST)
    return value, carry


def reference(iterate, residual, direction, prior_rho, diag_blocks, lower_coupling, upper_coupling, interface, jacobi_inverse, slab_inverse, lower_factor, upper_factor):
    shape3 = (NSLAB, B, R)
    iterate_s = iterate.reshape(shape3)
    residual_s = residual.reshape(shape3)
    direction_s = direction.reshape(shape3)
    diag_s = diag_blocks.reshape(NSLAB, B, B)
    lower_s = lower_coupling.reshape(NSLAB, B, IF)
    upper_s = upper_coupling.reshape(NSLAB, B, IF)
    image = operate(direction_s, diag_s, lower_s, upper_s, interface)
    curvature = jnp.sum(direction_s * image, axis=(0, 1))
    step_size = prior_rho / curvature
    new_iterate = iterate_s + step_size * direction_s
    new_residual = residual_s - step_size * image
    jacobi_s = jacobi_inverse.reshape(NSLAB * N_GRP, GB, GB)
    smoothed = slab_apply(jacobi_s, new_residual.reshape(NSLAB * N_GRP, GB, R)).reshape(shape3)
    defect = new_residual - operate(smoothed, diag_s, lower_s, upper_s, interface)
    inverse_s = slab_inverse.reshape(NSLAB, B, B)
    solved = slab_apply(inverse_s, defect)
    factor = slab_apply(inverse_s, lower_factor.reshape(NSLAB, B, IF))
    offsets = pick_rows(solved, interface)
    transfer = -pick_rows(factor, interface)
    upper_f = upper_factor.reshape(NSLAB, B, IF)
    upper_iface = -pick_rows(upper_f, interface)
    start = jnp.zeros((IF, R), jnp.float32)
    _, forward_prev = lax.scan(affine_step, start, (transfer, offsets))
    forward_vals = solved - slab_apply(factor, forward_prev)
    iface_vals = offsets + slab_apply(transfer, forward_prev)
    _, backward_next = lax.scan(affine_step, start, (upper_iface, iface_vals), reverse=True)
    correction = forward_vals - slab_apply(upper_f, backward_next)
    precond = smoothed + correction
    new_rho = jnp.sum(new_residual * precond, axis=(0, 1))
    new_direction = precond + (new_rho / prior_rho) * direction_s
    return (new_iterate.reshape(ROWS, R), new_residual.reshape(ROWS, R), new_direction.reshape(ROWS, R), new_rho)
```

```python
import functools

import jax
import jax.numpy as jnp
from jax import lax
from jax.experimental import pallas as pl
from jax.experimental.pallas import tpu as pltpu
from jax.sharding import PartitionSpec as P

MESH = pl.DeviceIdType.MESH
BF = jnp.bfloat16
F32 = jnp.float32
LANES = 128


def split(x):
    hi = x.astype(BF)
    return hi, (x - hi.astype(F32)).astype(BF)


def dot(a, b):
    return jnp.dot(a, b, preferred_element_type=F32)


def mm(ah, al, b):
    bh, bl = split(b)
    width = b.shape[1]
    both = dot(ah, jnp.concatenate([bh, bl], axis=1))
    return both[:, :width] + (both[:, width:] + dot(al, bh))


def pick(sel, b):
    bh, bl = split(b)
    width = b.shape[1]
    both = dot(sel, jnp.concatenate([bh, bl], axis=1))
    return both[:, :width] + both[:, width:]


def each(low, high, fn):
    if high - low <= 16:
        for i in range(low, high):
            fn(i)
    else:
        lax.fori_loop(low, high, lambda i, c: (fn(i), c)[1], 0)


def kernel(
    ns, ng, nh,
    it_ref, res_ref, dir_ref, rho_ref, diag_ref, low_ref, up_ref, idx_ref, jac_ref, inv_ref, lf_ref, uf_ref,
    out_it, out_res, out_dir, out_rho,
    dfull, rfull, diagf, lowf, upf, jacf, invf, lff, uff,
    mh, ml, ih, il,
    face_out, face_in, tu, offs, fps, fback,
    sbuf, sums, rows_out, rows_in,
    m_send, m_recv, f_send, f_recv, t_send, t_recv, s_send, s_recv, r_send, r_recv,
):
    k = lax.axis_index("slab")
    g = lax.axis_index("grp")
    h = lax.rem(g, nh)
    base = g - h
    gb = dir_ref.shape[0]
    B = gb * ng
    IF = idx_ref.shape[1]

    def dev(slab, grp):
        return {"slab": slab, "grp": grp}

    def signal_slab(off):
        for j in range(nh):
            pl.semaphore_signal(bar, inc=1, device_id=dev(lax.rem(k + off, ns), base + j), device_id_type=MESH)

    bar = pltpu.get_barrier_semaphore()
    for off in range(1, ng):
        pl.semaphore_signal(bar, inc=1, device_id=dev(k, lax.rem(g + off, ng)), device_id_type=MESH)
    each(1, ns, signal_slab)
    pl.semaphore_wait(bar, (ng - 1) + (ns - 1) * nh)

    mine = pl.ds(pl.multiple_of(g * gb, 8), gb)

    mats = [
        (dir_ref, dfull), (diag_ref, diagf), (res_ref, rfull), (jac_ref, jacf), (low_ref, lowf), (up_ref, upf),
        (inv_ref, invf), (lf_ref, lff), (uf_ref, uff),
    ]
    D, DIAG, RES, JAC, LOW, UP, INV, LF, UF = range(9)

    def mat_copy(m, off):
        ref, full = mats[m]
        peer = lax.rem(g + off, ng)
        if m in (D, RES):
            src = ref.at[:, pl.ds(pl.multiple_of(lax.rem(peer, nh) * LANES, LANES), LANES)]
        else:
            src = ref
        return pltpu.make_async_remote_copy(
            src_ref=src, dst_ref=full.at[mine, :], send_sem=m_send.at[m, off], recv_sem=m_recv.at[m, off],
            device_id=dev(k, peer), device_id_type=MESH)

    for m in range(len(mats)):
        for off in range(1, ng):
            mat_copy(m, off).start()

    half = pl.ds(pl.multiple_of(h * LANES, LANES), LANES)
    dfull[mine, :] = dir_ref[:, half]
    rfull[mine, :] = res_ref[:, half]
    for m in range(len(mats)):
        if m not in (D, RES):
            mats[m][1][mine, :] = mats[m][0][...]

    def arrived(m):
        for off in range(1, ng):
            mat_copy(m, off).wait_recv()

    sel = jnp.transpose(
        (lax.broadcasted_iota(jnp.int32, (B, IF), 0) == idx_ref[...]).astype(F32)).astype(BF)

    def face_copy(slot, side):
        to = k + 1 if side == 0 else k - 1
        return pltpu.make_async_remote_copy(
            src_ref=face_out.at[slot], dst_ref=face_in.at[slot, side], send_sem=f_send.at[slot, side],
            recv_sem=f_recv.at[slot, side], device_id=dev(to, g), device_id_type=MESH)

    def send_face(slot, value):
        face_out[slot] = value

        @pl.when(k < ns - 1)
        def _():
            face_copy(slot, 0).start()

        @pl.when(k > 0)
        def _():
            face_copy(slot, 1).start()

    def wait_face(slot):
        @pl.when(k > 0)
        def _():
            face_copy(slot, 0).wait_recv()

        @pl.when(k < ns - 1)
        def _():
            face_copy(slot, 1).wait_recv()

    @pl.when(k == 0)
    def _():
        for slot in range(3):
            face_in[slot, 0] = jnp.zeros((IF, LANES), F32)

    @pl.when(k == ns - 1)
    def _():
        for slot in range(3):
            face_in[slot, 1] = jnp.zeros((IF, LANES), F32)

    def jacobi(field):
        return jnp.concatenate(
            [mm(*split(jacf[j * gb:(j + 1) * gb, :]), field[j * gb:(j + 1) * gb, :]) for j in range(ng)], axis=0)

    arrived(D)
    d = dfull[...]
    send_face(0, pick(sel, d))
    arrived(DIAG)
    mh[:, :B], ml[:, :B] = split(diagf[...])
    arrived(RES)
    arrived(JAC)
    r = rfull[...]
    jr = jacobi(r)
    send_face(1, pick(sel, jr))
    image = mm(mh[:, :B], ml[:, :B], d)
    arrived(LOW)
    mh[:, B:B + IF], ml[:, B:B + IF] = split(lowf[...])
    arrived(UP)
    mh[:, B + IF:], ml[:, B + IF:] = split(upf[...])
    wait_face(0)
    image = image + mm(mh[:, B:], ml[:, B:], jnp.concatenate([face_in[0, 0], face_in[0, 1]], axis=0))

    def sum_copy(which, off, j):
        to = lax.rem(k + off, ns)
        flat = off * nh + lax.rem(j + nh - h, nh)
        return pltpu.make_async_remote_copy(
            src_ref=sbuf.at[which], dst_ref=sums.at[which, k * nh + h], send_sem=s_send.at[which, flat],
            recv_sem=s_recv.at[which, flat], device_id=dev(to, base + j), device_id_type=MESH)

    def sum_desc(which, off, turn):
        flat = off * nh + turn
        frm_k = lax.rem(k + ns - off, ns)
        frm_h = lax.rem(h + nh - turn, nh)
        return pltpu.make_async_remote_copy(
            src_ref=sbuf.at[which], dst_ref=sums.at[which, frm_k * nh + frm_h], send_sem=s_send.at[which, flat],
            recv_sem=s_recv.at[which, flat], device_id=dev(lax.rem(k + off, ns), base + lax.rem(h + turn, nh)),
            device_id_type=MESH)

    def sum_send(which, value):
        sbuf[which] = value
        sums[which, k * nh + h] = value

        def go(off):
            for turn in range(nh):
                if isinstance(off, int) and off == 0 and turn == 0:
                    continue
                flat = off * nh + turn
                pltpu.make_async_remote_copy(
                    src_ref=sbuf.at[which], dst_ref=sums.at[which, k * nh + h], send_sem=s_send.at[which, flat],
                    recv_sem=s_recv.at[which, flat],
                    device_id=dev(lax.rem(k + off, ns), base + lax.rem(h + turn, nh)), device_id_type=MESH).start()

        go(0)
        each(1, ns, go)

    def sum_wait(which, turn):
        if turn != 0:
            sum_desc(which, 0, turn).wait_recv()
        each(1, ns, lambda off: sum_desc(which, off, turn).wait_recv())

    def total(which, j):
        return lax.fori_loop(
            0, ns, lambda i, acc: acc + sums[which, i * nh + j], jnp.zeros((1, LANES), F32))

    sum_send(0, jnp.sum(d * image, axis=0, keepdims=True))
    jim = jacobi(image)
    send_face(2, pick(sel, jim))

    def tu_copy(which, off):
        return pltpu.make_async_remote_copy(
            src_ref=tu.at[which, k], dst_ref=tu.at[which, k], send_sem=t_send.at[which, off],
            recv_sem=t_recv.at[which, off], device_id=dev(lax.rem(k + off, ns), g), device_id_type=MESH)

    def tu_wait(which, off):
        frm = lax.rem(k + ns - off, ns)
        pltpu.make_async_remote_copy(
            src_ref=tu.at[which, frm], dst_ref=tu.at[which, frm], send_sem=t_send.at[which, off],
            recv_sem=t_recv.at[which, off], device_id=dev(lax.rem(k + off, ns), g),
            device_id_type=MESH).wait_recv()

    arrived(INV)
    ih[:B, :], il[:B, :] = split(invf[...])
    ih[B:, :] = dot(sel, ih[:B, :]).astype(BF)
    il[B:, :] = dot(sel, il[:B, :]).astype(BF)
    arrived(LF)
    factor = mm(ih[...], il[...], lff[...])
    tu[0, k] = -factor[B:, :]
    each(1, ns, lambda off: tu_copy(0, off).start())
    fback[:, :IF] = factor[:B, :]
    arrived(UF)
    tu[1, k] = -pick(sel, uff[...])
    each(1, ns, lambda off: tu_copy(1, off).start())
    fback[:, IF:] = uff[...]

    rho = rho_ref[0:1, half]
    sum_wait(0, 0)
    alpha = rho / total(0, h)
    rn = r - alpha * image

    def rows_copy(which, turn):
        to = base + lax.rem(h + turn, nh)
        return pltpu.make_async_remote_copy(
            src_ref=rows_out.at[which, pl.ds(pl.multiple_of(to * gb, 8), gb), :], dst_ref=rows_in.at[which, turn],
            send_sem=r_send.at[which, turn], recv_sem=r_recv.at[which, turn], device_id=dev(k, to),
            device_id_type=MESH)

    rows_out[0] = rn
    for turn in range(1, nh):
        rows_copy(0, turn).start()
    wait_face(1)
    wait_face(2)
    s = jr - alpha * jim
    faces = jnp.concatenate(
        [s] + [face_in[1, side] - alpha * face_in[2, side] for side in range(2)], axis=0)
    defect = rn - mm(mh[...], ml[...], faces)
    both = mm(ih[...], il[...], defect)
    solved = both[:B, :]
    tu[2, k] = both[B:, :]
    each(1, ns, lambda off: tu_copy(2, off).start())

    for which in range(3):
        each(1, ns, functools.partial(tu_wait, which))

    def forward(i, prev):
        fps[i] = prev
        return tu[2, i] + mm(*split(tu[0, i]), prev)

    last = lax.fori_loop(0, ns, forward, jnp.zeros((IF, LANES), F32), unroll=ns <= 8)
    fps[ns] = last

    def backward(t, nxt):
        i = ns - 1 - t
        offs[i] = nxt
        return fps[i + 1] + mm(*split(tu[1, i]), nxt)

    lax.fori_loop(0, ns, backward, jnp.zeros((IF, LANES), F32), unroll=ns <= 8)
    ends = jnp.concatenate([fps[k], offs[k]], axis=0)
    precond = s + (solved - mm(*split(fback[...]), ends))
    rows_out[1] = precond
    for turn in range(1, nh):
        rows_copy(1, turn).start()
    sum_send(1, jnp.sum(rn * precond, axis=0, keepdims=True))

    def put(j_half, alpha_j, res_rows, turn):
        cols = pl.ds(pl.multiple_of(j_half * LANES, LANES), LANES)
        out_it[:, cols] = it_ref[:, cols] + alpha_j * dir_ref[:, cols]
        out_res[:, cols] = res_rows

    put(h, alpha, rows_out[0, mine, :], 0)
    for turn in range(1, nh):
        sum_wait(0, turn)
        j = lax.rem(h + nh - turn, nh)
        rows_copy(0, turn).wait_recv()
        cols = pl.ds(pl.multiple_of(j * LANES, LANES), LANES)
        put(j, rho_ref[0:1, cols] / total(0, j), rows_in[0, turn], turn)

    for turn in range(nh):
        sum_wait(1, turn)
        j = lax.rem(h + nh - turn, nh)
        cols = pl.ds(pl.multiple_of(j * LANES, LANES), LANES)
        new = total(1, j)
        out_rho[0:1, cols] = new
        if turn:
            rows_copy(1, turn).wait_recv()
            part = rows_in[1, turn]
        else:
            part = rows_out[1, mine, :]
        out_dir[:, cols] = part + new / rho_ref[0:1, cols] * dir_ref[:, cols]

    for m in range(len(mats)):
        for off in range(1, ng):
            mat_copy(m, off).wait_send()
    for slot in range(3):
        @pl.when(k < ns - 1)
        def _():
            face_copy(slot, 0).wait_send()

        @pl.when(k > 0)
        def _():
            face_copy(slot, 1).wait_send()
    for which in range(3):
        each(1, ns, lambda off: tu_copy(which, off).wait_send())
    for which in range(2):
        for turn in range(1, nh):
            rows_copy(which, turn).wait_send()
            sum_desc(which, 0, turn).wait_send()
        for turn in range(nh):
            each(1, ns, lambda off: sum_desc(which, off, turn).wait_send())


def local(ns, ng, iterate, residual, direction, prior_rho, *rest):
    gb, cols = direction.shape
    nh = cols // LANES
    B = gb * ng
    IF = rest[1].shape[1]
    row = jax.ShapeDtypeStruct((gb, cols), F32)
    V = pltpu.VMEM
    DMA = pltpu.SemaphoreType.DMA
    vm = pl.BlockSpec(memory_space=pltpu.VMEM)
    out = pl.pallas_call(
        functools.partial(kernel, ns, ng, nh),
        out_shape=(row, row, row, jax.ShapeDtypeStruct((1, cols), F32)),
        in_specs=[vm] * 12,
        out_specs=(vm,) * 4,
        scratch_shapes=[
            V((B, LANES), F32), V((B, LANES), F32), V((B, B), F32), V((B, IF), F32), V((B, IF), F32),
            V((B, gb), F32), V((B, B), F32), V((B, IF), F32), V((B, IF), F32),
            V((B, B + 2 * IF), BF), V((B, B + 2 * IF), BF), V((B + IF, B), BF), V((B + IF, B), BF),
            V((3, IF, LANES), F32), V((3, 2, IF, LANES), F32), V((3, ns, IF, LANES), F32),
            V((ns, IF, LANES), F32), V((ns + 1, IF, LANES), F32), V((B, 2 * IF), F32),
            V((2, 1, LANES), F32), V((2, ns * nh, 1, LANES), F32),
            V((2, B, LANES), F32), V((2, nh, gb, LANES), F32),
            DMA((9, ng)), DMA((9, ng)), DMA((3, 2)), DMA((3, 2)), DMA((3, ns)), DMA((3, ns)),
            DMA((2, ns * nh)), DMA((2, ns * nh)), DMA((2, nh)), DMA((2, nh)),
        ],
        compiler_params=pltpu.CompilerParams(
            collective_id=0, has_side_effects=True, vmem_limit_bytes=60 * 1024 * 1024),
    )(iterate, residual, direction, prior_rho.reshape(1, cols), *rest)
    return out[0], out[1], out[2], out[3].reshape(cols)


def solution(mesh):
    rows = P(("slab", "grp"), None)
    in_specs = (rows, rows, rows, P(), rows, rows, rows, P("slab", None), rows, rows, rows, rows)
    out_specs = (rows, rows, rows, P())
    body = functools.partial(local, mesh.shape["slab"], mesh.shape["grp"])
    return jax.shard_map(body, mesh=mesh, in_specs=in_specs, out_specs=out_specs, check_vma=False)
```

```python
import functools

import jax
import jax.numpy as jnp
from jax import lax
from jax.experimental import pallas as pl
from jax.experimental.pallas import tpu as pltpu
from jax.sharding import PartitionSpec as P

MESH = pl.DeviceIdType.MESH
BF = jnp.bfloat16
F32 = jnp.float32
LANES = 128


def split(x):
    hi = x.astype(BF)
    return hi, (x - hi.astype(F32)).astype(BF)


def dot(a, b):
    return jnp.dot(a, b, preferred_element_type=F32)


def mm(ah, al, b):
    bh, bl = split(b)
    width = b.shape[1]
    both = dot(ah, jnp.concatenate([bh, bl], axis=1))
    return both[:, :width] + (both[:, width:] + dot(al, bh))


def pick(sel, b):
    bh, bl = split(b)
    width = b.shape[1]
    both = dot(sel, jnp.concatenate([bh, bl], axis=1))
    return both[:, :width] + both[:, width:]


def each(low, high, fn):
    if high - low <= 16:
        for i in range(low, high):
            fn(i)
    else:
        lax.fori_loop(low, high, lambda i, c: (fn(i), c)[1], 0)


def kernel(
    ns, ng, nh,
    it_ref, res_ref, dir_ref, rho_ref, diag_ref, low_ref, up_ref, idx_ref, jac_ref, inv_ref, lf_ref, uf_ref,
    out_it, out_res, out_dir, out_rho,
    dfull, rfull, diagf, lowf, upf, jacf, invf, lff, uff,
    mh, ml, ih, il,
    face_out, face_in, tu, offs, fps, fback, fown, ffull,
    sbuf, sums, rows_out, rows_in,
    m_send, m_recv, f_send, f_recv, t_send, t_recv, s_send, s_recv, r_send, r_recv, x_send, x_recv,
):
    k = lax.axis_index("slab")
    g = lax.axis_index("grp")
    h = lax.rem(g, nh)
    base = g - h
    gb = dir_ref.shape[0]
    B = gb * ng
    IF = idx_ref.shape[1]

    def dev(slab, grp):
        return {"slab": slab, "grp": grp}

    def signal_slab(off):
        for j in range(nh):
            pl.semaphore_signal(bar, inc=1, device_id=dev(lax.rem(k + off, ns), base + j), device_id_type=MESH)

    bar = pltpu.get_barrier_semaphore()
    for off in range(1, ng):
        pl.semaphore_signal(bar, inc=1, device_id=dev(k, lax.rem(g + off, ng)), device_id_type=MESH)
    each(1, ns, signal_slab)
    pl.semaphore_wait(bar, (ng - 1) + (ns - 1) * nh)

    mine = pl.ds(pl.multiple_of(g * gb, 8), gb)

    mats = [
        (dir_ref, dfull), (diag_ref, diagf), (res_ref, rfull), (jac_ref, jacf), (low_ref, lowf), (up_ref, upf),
        (inv_ref, invf), (lf_ref, lff), (uf_ref, uff), (fown, ffull),
    ]
    D, DIAG, RES, JAC, LOW, UP, INV, LF, UF, FAC = range(10)

    def mat_copy(m, flat):
        ref, full = mats[m]
        away, turn = flat // nh, flat % nh
        if m in (D, RES):
            peer = lax.rem(g + flat, ng)
            src, dst = ref.at[:, pl.ds(pl.multiple_of(lax.rem(peer, nh) * LANES, LANES), LANES)], mine
        elif turn == 0:
            peer = lax.rem(g + away * nh, ng)
            src, dst = ref, mine
        else:
            peer = base + lax.rem(h + turn, nh)
            owner = lax.rem(g + ng - away * nh, ng)
            dst = pl.ds(pl.multiple_of(owner * gb, 8), gb)
            src = ref if away == 0 else full.at[dst, :]
        return pltpu.make_async_remote_copy(
            src_ref=src, dst_ref=full.at[dst, :], send_sem=m_send.at[m, flat], recv_sem=m_recv.at[m, flat],
            device_id=dev(k, peer), device_id_type=MESH)

    def start(m):
        for flat in range(1, ng):
            if m in (D, RES) or flat < nh or flat % nh == 0:
                mat_copy(m, flat).start()

    for m in (LF, D, UF):
        start(m)

    def hand_on(m):
        for away in range(1, ng // nh):
            mat_copy(m, away * nh).wait_recv()
            for turn in range(1, nh):
                mat_copy(m, away * nh + turn).start()

    half = pl.ds(pl.multiple_of(h * LANES, LANES), LANES)
    dfull[mine, :] = dir_ref[:, half]
    rfull[mine, :] = res_ref[:, half]
    for m in range(len(mats)):
        if m not in (D, RES, FAC):
            mats[m][1][mine, :] = mats[m][0][...]

    def arrived(m):
        for flat in range(1, ng):
            if m in (D, RES) or flat < nh or flat % nh:
                mat_copy(m, flat).wait_recv()

    sel = jnp.transpose(
        (lax.broadcasted_iota(jnp.int32, (B, IF), 0) == idx_ref[...]).astype(F32)).astype(BF)

    def face_copy(slot, side):
        to = k + 1 if side == 0 else k - 1
        return pltpu.make_async_remote_copy(
            src_ref=face_out.at[slot], dst_ref=face_in.at[slot, side], send_sem=f_send.at[slot, side],
            recv_sem=f_recv.at[slot, side], device_id=dev(to, g), device_id_type=MESH)

    def send_face(slot, value):
        face_out[slot] = value

        @pl.when(k < ns - 1)
        def _():
            face_copy(slot, 0).start()

        @pl.when(k > 0)
        def _():
            face_copy(slot, 1).start()

    def wait_face(slot):
        @pl.when(k > 0)
        def _():
            face_copy(slot, 0).wait_recv()

        @pl.when(k < ns - 1)
        def _():
            face_copy(slot, 1).wait_recv()

    @pl.when(k == 0)
    def _():
        for slot in range(3):
            face_in[slot, 0] = jnp.zeros((IF, LANES), F32)

    @pl.when(k == ns - 1)
    def _():
        for slot in range(3):
            face_in[slot, 1] = jnp.zeros((IF, LANES), F32)

    def jacobi(field):
        return jnp.concatenate(
            [mm(*split(jacf[j * gb:(j + 1) * gb, :]), field[j * gb:(j + 1) * gb, :]) for j in range(ng)], axis=0)

    share = IF // nh
    own_share = pl.ds(pl.multiple_of(h * share, 8), share)

    nb = ng // nh
    g_share = IF // nb
    group_share = pl.ds(pl.multiple_of(g // nh * g_share, 8), g_share)
    passes = (nh, nh, nb)

    def tu_at(which, slab):
        return tu.at[which, slab, group_share if which == 2 else own_share, :]

    def tu_copy(which, off):
        return pltpu.make_async_remote_copy(
            src_ref=tu_at(which, k), dst_ref=tu_at(which, k), send_sem=t_send.at[which, off],
            recv_sem=t_recv.at[which, off], device_id=dev(lax.rem(k + off, ns), g), device_id_type=MESH)

    def tu_wait(which, off):
        frm = lax.rem(k + ns - off, ns)
        pltpu.make_async_remote_copy(
            src_ref=tu_at(which, frm), dst_ref=tu_at(which, frm), send_sem=t_send.at[which, off],
            recv_sem=t_recv.at[which, off], device_id=dev(lax.rem(k + off, ns), g),
            device_id_type=MESH).wait_recv()

    def tu_pass(which, turn, off):
        to = lax.rem(g + turn * nh, ng) if which == 2 else base + lax.rem(h + turn, nh)
        frm = lax.rem(k + ns - off, ns)
        return pltpu.make_async_remote_copy(
            src_ref=tu_at(which, frm), dst_ref=tu_at(which, frm), send_sem=x_send.at[which, turn, off],
            recv_sem=x_recv.at[which, turn, off], device_id=dev(k, to), device_id_type=MESH)

    def tu_hand_on(which, off):
        tu_wait(which, off)
        for turn in range(1, passes[which]):
            tu_pass(which, turn, off).start()

    hand_on(LF)
    arrived(LF)
    fown[...] = mm(*split(inv_ref[...]), lff[...])
    ffull[mine, :] = fown[...]
    for m in (FAC, DIAG, LOW, UP, RES, JAC, INV):
        start(m)

    arrived(D)
    d = dfull[...]
    send_face(0, pick(sel, d))
    hand_on(UF)
    arrived(UF)
    tu[1, k] = -pick(sel, uff[...])
    each(1, ns, lambda off: tu_copy(1, off).start())
    fback[:, IF:] = uff[...]
    hand_on(FAC)
    arrived(FAC)
    tu[0, k] = -pick(sel, ffull[...])
    each(1, ns, lambda off: tu_copy(0, off).start())
    fback[:, :IF] = ffull[...]

    hand_on(DIAG)
    hand_on(LOW)
    hand_on(UP)
    arrived(DIAG)
    mh[:, :B], ml[:, :B] = split(diagf[...])
    image = mm(mh[:, :B], ml[:, :B], d)
    arrived(LOW)
    mh[:, B:B + IF], ml[:, B:B + IF] = split(lowf[...])
    arrived(UP)
    mh[:, B + IF:], ml[:, B + IF:] = split(upf[...])
    wait_face(0)
    image = image + mm(mh[:, B:], ml[:, B:], jnp.concatenate([face_in[0, 0], face_in[0, 1]], axis=0))

    def sum_desc(which, off, turn):
        flat = off * nh + turn
        frm_k = lax.rem(k + ns - off, ns)
        frm_h = lax.rem(h + nh - turn, nh)
        return pltpu.make_async_remote_copy(
            src_ref=sbuf.at[which], dst_ref=sums.at[which, frm_k * nh + frm_h], send_sem=s_send.at[which, flat],
            recv_sem=s_recv.at[which, flat], device_id=dev(lax.rem(k + off, ns), base + lax.rem(h + turn, nh)),
            device_id_type=MESH)

    def sum_send(which, value):
        sbuf[which] = value
        sums[which, k * nh + h] = value

        def go(off):
            for turn in range(nh):
                if isinstance(off, int) and off == 0 and turn == 0:
                    continue
                flat = off * nh + turn
                pltpu.make_async_remote_copy(
                    src_ref=sbuf.at[which], dst_ref=sums.at[which, k * nh + h], send_sem=s_send.at[which, flat],
                    recv_sem=s_recv.at[which, flat],
                    device_id=dev(lax.rem(k + off, ns), base + lax.rem(h + turn, nh)), device_id_type=MESH).start()

        go(0)
        each(1, ns, go)

    def sum_wait(which, turn):
        if turn != 0:
            sum_desc(which, 0, turn).wait_recv()
        each(1, ns, lambda off: sum_desc(which, off, turn).wait_recv())

    def total(which, j):
        return lax.fori_loop(
            0, ns, lambda i, acc: acc + sums[which, i * nh + j], jnp.zeros((1, LANES), F32))

    sum_send(0, jnp.sum(d * image, axis=0, keepdims=True))
    arrived(RES)
    hand_on(JAC)
    arrived(JAC)
    r = rfull[...]
    smooth = jacobi(jnp.concatenate([r, image], axis=1))
    jr, jim = smooth[:, :LANES], smooth[:, LANES:]
    send_face(1, pick(sel, jr))
    send_face(2, pick(sel, jim))

    hand_on(INV)
    arrived(INV)
    ih[:B, :], il[:B, :] = split(invf[...])
    ih[B:, :] = dot(sel, ih[:B, :]).astype(BF)
    il[B:, :] = dot(sel, il[:B, :]).astype(BF)

    rho = rho_ref[0:1, half]
    sum_wait(0, 0)
    alpha = rho / total(0, h)
    rn = r - alpha * image

    def rows_copy(which, turn):
        to = base + lax.rem(h + turn, nh)
        return pltpu.make_async_remote_copy(
            src_ref=rows_out.at[which, pl.ds(pl.multiple_of(to * gb, 8), gb), :], dst_ref=rows_in.at[which, turn],
            send_sem=r_send.at[which, turn], recv_sem=r_recv.at[which, turn], device_id=dev(k, to),
            device_id_type=MESH)

    rows_out[0] = rn
    for turn in range(1, nh):
        rows_copy(0, turn).start()
    wait_face(1)
    wait_face(2)
    s = jr - alpha * jim
    faces = jnp.concatenate(
        [s] + [face_in[1, side] - alpha * face_in[2, side] for side in range(2)], axis=0)
    defect = rn - mm(mh[...], ml[...], faces)
    both = mm(ih[...], il[...], defect)
    solved = both[:B, :]
    tu[2, k] = both[B:, :]
    each(1, ns, lambda off: tu_copy(2, off).start())

    for which in range(2):
        each(1, ns, functools.partial(tu_hand_on, which))
    each(1, ns, functools.partial(tu_hand_on, 2))
    for which in range(3):
        for turn in range(1, passes[which]):
            each(1, ns, lambda off: tu_pass(which, turn, off).wait_recv())

    def forward(i, prev):
        fps[i] = prev
        return tu[2, i] + mm(*split(tu[0, i]), prev)

    last = lax.fori_loop(0, ns, forward, jnp.zeros((IF, LANES), F32), unroll=ns <= 8)
    fps[ns] = last

    def backward(t, nxt):
        i = ns - 1 - t
        offs[i] = nxt
        return fps[i + 1] + mm(*split(tu[1, i]), nxt)

    lax.fori_loop(0, ns, backward, jnp.zeros((IF, LANES), F32), unroll=ns <= 8)
    ends = jnp.concatenate([fps[k], offs[k]], axis=0)
    precond = s + (solved - mm(*split(fback[...]), ends))
    rows_out[1] = precond
    for turn in range(1, nh):
        rows_copy(1, turn).start()
    sum_send(1, jnp.sum(rn * precond, axis=0, keepdims=True))

    def put(j_half, alpha_j, res_rows, turn):
        cols = pl.ds(pl.multiple_of(j_half * LANES, LANES), LANES)
        out_it[:, cols] = it_ref[:, cols] + alpha_j * dir_ref[:, cols]
        out_res[:, cols] = res_rows

    put(h, alpha, rows_out[0, mine, :], 0)
    for turn in range(1, nh):
        sum_wait(0, turn)
        j = lax.rem(h + nh - turn, nh)
        rows_copy(0, turn).wait_recv()
        cols = pl.ds(pl.multiple_of(j * LANES, LANES), LANES)
        put(j, rho_ref[0:1, cols] / total(0, j), rows_in[0, turn], turn)

    for turn in range(nh):
        sum_wait(1, turn)
        j = lax.rem(h + nh - turn, nh)
        cols = pl.ds(pl.multiple_of(j * LANES, LANES), LANES)
        new = total(1, j)
        out_rho[0:1, cols] = new
        if turn:
            rows_copy(1, turn).wait_recv()
            part = rows_in[1, turn]
        else:
            part = rows_out[1, mine, :]
        out_dir[:, cols] = part + new / rho_ref[0:1, cols] * dir_ref[:, cols]

    for m in range(len(mats)):
        for off in range(1, ng):
            mat_copy(m, off).wait_send()
    for slot in range(3):
        @pl.when(k < ns - 1)
        def _():
            face_copy(slot, 0).wait_send()

        @pl.when(k > 0)
        def _():
            face_copy(slot, 1).wait_send()
    for which in range(3):
        each(1, ns, lambda off: tu_copy(which, off).wait_send())
        for turn in range(1, passes[which]):
            each(1, ns, lambda off: tu_pass(which, turn, off).wait_send())
    for which in range(2):
        for turn in range(1, nh):
            rows_copy(which, turn).wait_send()
            sum_desc(which, 0, turn).wait_send()
        for turn in range(nh):
            each(1, ns, lambda off: sum_desc(which, off, turn).wait_send())


def local(ns, ng, iterate, residual, direction, prior_rho, *rest):
    gb, cols = direction.shape
    nh = cols // LANES
    B = gb * ng
    IF = rest[1].shape[1]
    row = jax.ShapeDtypeStruct((gb, cols), F32)
    V = pltpu.VMEM
    DMA = pltpu.SemaphoreType.DMA
    vm = pl.BlockSpec(memory_space=pltpu.VMEM)
    out = pl.pallas_call(
        functools.partial(kernel, ns, ng, nh),
        out_shape=(row, row, row, jax.ShapeDtypeStruct((1, cols), F32)),
        in_specs=[vm] * 12,
        out_specs=(vm,) * 4,
        scratch_shapes=[
            V((B, LANES), F32), V((B, LANES), F32), V((B, B), F32), V((B, IF), F32), V((B, IF), F32),
            V((B, gb), F32), V((B, B), F32), V((B, IF), F32), V((B, IF), F32),
            V((B, B + 2 * IF), BF), V((B, B + 2 * IF), BF), V((B + IF, B), BF), V((B + IF, B), BF),
            V((3, IF, LANES), F32), V((3, 2, IF, LANES), F32), V((3, ns, IF, LANES), F32),
            V((ns, IF, LANES), F32), V((ns + 1, IF, LANES), F32), V((B, 2 * IF), F32), V((gb, IF), F32), V((B, IF), F32),
            V((2, 1, LANES), F32), V((2, ns * nh, 1, LANES), F32),
            V((2, B, LANES), F32), V((2, nh, gb, LANES), F32),
            DMA((10, ng)), DMA((10, ng)), DMA((3, 2)), DMA((3, 2)), DMA((3, ns)), DMA((3, ns)),
            DMA((2, ns * nh)), DMA((2, ns * nh)), DMA((2, nh)), DMA((2, nh)), DMA((3, max(nh, ng // nh), ns)), DMA((3, max(nh, ng // nh), ns)),
        ],
        compiler_params=pltpu.CompilerParams(
            collective_id=0, has_side_effects=True, vmem_limit_bytes=60 * 1024 * 1024),
    )(iterate, residual, direction, prior_rho.reshape(1, cols), *rest)
    return out[0], out[1], out[2], out[3].reshape(cols)


def solution(mesh):
    rows = P(("slab", "grp"), None)
    in_specs = (rows, rows, rows, P(), rows, rows, rows, P("slab", None), rows, rows, rows, rows)
    out_specs = (rows, rows, rows, P())
    body = functools.partial(local, mesh.shape["slab"], mesh.shape["grp"])
    return jax.shard_map(body, mesh=mesh, in_specs=in_specs, out_specs=out_specs, check_vma=False)
```

```python
import functools

import jax
import jax.numpy as jnp
from jax import lax
from jax.experimental import pallas as pl
from jax.experimental.pallas import tpu as pltpu
from jax.sharding import PartitionSpec as P

MESH = pl.DeviceIdType.MESH
BF = jnp.bfloat16
F32 = jnp.float32
LANES = 128


def split(x):
    hi = x.astype(BF)
    return hi, (x - hi.astype(F32)).astype(BF)


def dot(a, b):
    return jnp.dot(a, b, preferred_element_type=F32)


def mm(ah, al, b):
    bh, bl = split(b)
    width = b.shape[1]
    both = dot(ah, jnp.concatenate([bh, bl], axis=1))
    return both[:, :width] + (both[:, width:] + dot(al, bh))


def pick(sel, b):
    bh, bl = split(b)
    width = b.shape[1]
    both = dot(sel, jnp.concatenate([bh, bl], axis=1))
    return both[:, :width] + both[:, width:]


def each(low, high, fn):
    if high - low <= 16:
        for i in range(low, high):
            fn(i)
    else:
        lax.fori_loop(low, high, lambda i, c: (fn(i), c)[1], 0)


def kernel(
    ns, ng, nh,
    it_hbm, res_hbm, dir_hbm, rho_ref, diag_hbm, low_hbm, up_hbm, idx_ref, jac_hbm, inv_hbm, lf_hbm, uf_hbm,
    out_it, out_res, out_dir, out_rho,
    dfull, rfull, diagf, lowf, upf, jacf, invf, lff, uff,
    mh, ml, ih, il,
    face_out, face_in, tu, offs, fps, fback, fown, ffull,
    it_ref, res_ref, dir_ref, diag_ref, low_ref, up_ref, jac_ref, inv_ref, lf_ref, uf_ref, in_sem,
    sbuf, sums, rows_out, rows_in,
    m_send, m_recv, f_send, f_recv, t_send, t_recv, s_send, s_recv, r_send, r_recv, x_send, x_recv,
):
    k = lax.axis_index("slab")
    g = lax.axis_index("grp")
    h = lax.rem(g, nh)
    base = g - h
    gb = dir_ref.shape[0]
    B = gb * ng
    IF = idx_ref.shape[1]

    def dev(slab, grp):
        return {"slab": slab, "grp": grp}

    def signal_slab(off):
        for j in range(nh):
            pl.semaphore_signal(bar, inc=1, device_id=dev(lax.rem(k + off, ns), base + j), device_id_type=MESH)

    bar = pltpu.get_barrier_semaphore()
    for off in range(1, ng):
        pl.semaphore_signal(bar, inc=1, device_id=dev(k, lax.rem(g + off, ng)), device_id_type=MESH)
    each(1, ns, signal_slab)
    stage = [
        pltpu.make_async_copy(src, dst, in_sem.at[i]) for i, (src, dst) in enumerate((
            (lf_hbm, lf_ref), (dir_hbm, dir_ref), (uf_hbm, uf_ref), (inv_hbm, inv_ref), (diag_hbm, diag_ref),
            (low_hbm, low_ref), (up_hbm, up_ref), (res_hbm, res_ref), (jac_hbm, jac_ref), (it_hbm, it_ref)))]
    for copy in stage:
        copy.start()
    for copy in stage:
        copy.wait()
    pl.semaphore_wait(bar, (ng - 1) + (ns - 1) * nh)

    mine = pl.ds(pl.multiple_of(g * gb, 8), gb)

    mats = [
        (dir_ref, dfull), (diag_ref, diagf), (res_ref, rfull), (jac_ref, jacf), (low_ref, lowf), (up_ref, upf),
        (inv_ref, invf), (lf_ref, lff), (uf_ref, uff), (fown, ffull),
    ]
    D, DIAG, RES, JAC, LOW, UP, INV, LF, UF, FAC = range(10)

    def mat_copy(m, flat):
        ref, full = mats[m]
        away, turn = flat // nh, flat % nh
        if m in (D, RES):
            peer = lax.rem(g + flat, ng)
            src, dst = ref.at[:, pl.ds(pl.multiple_of(lax.rem(peer, nh) * LANES, LANES), LANES)], mine
        elif turn == 0:
            peer = lax.rem(g + away * nh, ng)
            src, dst = ref, mine
        else:
            peer = base + lax.rem(h + turn, nh)
            owner = lax.rem(g + ng - away * nh, ng)
            dst = pl.ds(pl.multiple_of(owner * gb, 8), gb)
            src = ref if away == 0 else full.at[dst, :]
        return pltpu.make_async_remote_copy(
            src_ref=src, dst_ref=full.at[dst, :], send_sem=m_send.at[m, flat], recv_sem=m_recv.at[m, flat],
            device_id=dev(k, peer), device_id_type=MESH)

    def start(m):
        for flat in range(1, ng):
            if m in (D, RES) or flat < nh or flat % nh == 0:
                mat_copy(m, flat).start()

    for m in (LF, D, UF):
        start(m)

    def hand_on(m):
        for away in range(1, ng // nh):
            mat_copy(m, away * nh).wait_recv()
            for turn in range(1, nh):
                mat_copy(m, away * nh + turn).start()

    half = pl.ds(pl.multiple_of(h * LANES, LANES), LANES)
    dfull[mine, :] = dir_ref[:, half]
    rfull[mine, :] = res_ref[:, half]
    for m in range(len(mats)):
        if m not in (D, RES, FAC):
            mats[m][1][mine, :] = mats[m][0][...]

    def arrived(m):
        for flat in range(1, ng):
            if m in (D, RES) or flat < nh or flat % nh:
                mat_copy(m, flat).wait_recv()

    sel = jnp.transpose(
        (lax.broadcasted_iota(jnp.int32, (B, IF), 0) == idx_ref[...]).astype(F32)).astype(BF)

    def face_copy(slot, side):
        to = k + 1 if side == 0 else k - 1
        return pltpu.make_async_remote_copy(
            src_ref=face_out.at[slot], dst_ref=face_in.at[slot, side], send_sem=f_send.at[slot, side],
            recv_sem=f_recv.at[slot, side], device_id=dev(to, g), device_id_type=MESH)

    def send_face(slot, value):
        face_out[slot] = value

        @pl.when(k < ns - 1)
        def _():
            face_copy(slot, 0).start()

        @pl.when(k > 0)
        def _():
            face_copy(slot, 1).start()

    def wait_face(slot):
        @pl.when(k > 0)
        def _():
            face_copy(slot, 0).wait_recv()

        @pl.when(k < ns - 1)
        def _():
            face_copy(slot, 1).wait_recv()

    @pl.when(k == 0)
    def _():
        for slot in range(3):
            face_in[slot, 0] = jnp.zeros((IF, LANES), F32)

    @pl.when(k == ns - 1)
    def _():
        for slot in range(3):
            face_in[slot, 1] = jnp.zeros((IF, LANES), F32)

    def jacobi(field):
        return jnp.concatenate(
            [mm(*split(jacf[j * gb:(j + 1) * gb, :]), field[j * gb:(j + 1) * gb, :]) for j in range(ng)], axis=0)

    share = IF // nh
    own_share = pl.ds(pl.multiple_of(h * share, 8), share)

    nb = ng // nh
    g_share = IF // nb
    group_share = pl.ds(pl.multiple_of(g // nh * g_share, 8), g_share)
    passes = (nh, nh, nb)

    def tu_at(which, slab):
        return tu.at[which, slab, group_share if which == 2 else own_share, :]

    def tu_copy(which, off):
        return pltpu.make_async_remote_copy(
            src_ref=tu_at(which, k), dst_ref=tu_at(which, k), send_sem=t_send.at[which, off],
            recv_sem=t_recv.at[which, off], device_id=dev(lax.rem(k + off, ns), g), device_id_type=MESH)

    def tu_wait(which, off):
        frm = lax.rem(k + ns - off, ns)
        pltpu.make_async_remote_copy(
            src_ref=tu_at(which, frm), dst_ref=tu_at(which, frm), send_sem=t_send.at[which, off],
            recv_sem=t_recv.at[which, off], device_id=dev(lax.rem(k + off, ns), g),
            device_id_type=MESH).wait_recv()

    def tu_pass(which, turn, off):
        to = lax.rem(g + turn * nh, ng) if which == 2 else base + lax.rem(h + turn, nh)
        frm = lax.rem(k + ns - off, ns)
        return pltpu.make_async_remote_copy(
            src_ref=tu_at(which, frm), dst_ref=tu_at(which, frm), send_sem=x_send.at[which, turn, off],
            recv_sem=x_recv.at[which, turn, off], device_id=dev(k, to), device_id_type=MESH)

    def tu_hand_on(which, off):
        tu_wait(which, off)
        for turn in range(1, passes[which]):
            tu_pass(which, turn, off).start()

    hand_on(LF)
    arrived(LF)
    fown[...] = mm(*split(inv_ref[...]), lff[...])
    ffull[mine, :] = fown[...]
    for m in (FAC, DIAG, LOW, UP, RES, JAC, INV):
        start(m)

    arrived(D)
    d = dfull[...]
    send_face(0, pick(sel, d))
    hand_on(UF)
    arrived(UF)
    tu[1, k] = -pick(sel, uff[...])
    each(1, ns, lambda off: tu_copy(1, off).start())
    fback[:, IF:] = uff[...]
    hand_on(FAC)
    arrived(FAC)
    tu[0, k] = -pick(sel, ffull[...])
    each(1, ns, lambda off: tu_copy(0, off).start())
    fback[:, :IF] = ffull[...]

    hand_on(DIAG)
    hand_on(LOW)
    hand_on(UP)
    arrived(DIAG)
    mh[:, :B], ml[:, :B] = split(diagf[...])
    image = mm(mh[:, :B], ml[:, :B], d)
    arrived(LOW)
    mh[:, B:B + IF], ml[:, B:B + IF] = split(lowf[...])
    arrived(UP)
    mh[:, B + IF:], ml[:, B + IF:] = split(upf[...])
    wait_face(0)
    image = image + mm(mh[:, B:], ml[:, B:], jnp.concatenate([face_in[0, 0], face_in[0, 1]], axis=0))

    def sum_desc(which, off, turn):
        flat = off * nh + turn
        frm_k = lax.rem(k + ns - off, ns)
        frm_h = lax.rem(h + nh - turn, nh)
        return pltpu.make_async_remote_copy(
            src_ref=sbuf.at[which], dst_ref=sums.at[which, frm_k * nh + frm_h], send_sem=s_send.at[which, flat],
            recv_sem=s_recv.at[which, flat], device_id=dev(lax.rem(k + off, ns), base + lax.rem(h + turn, nh)),
            device_id_type=MESH)

    def sum_send(which, value):
        sbuf[which] = value
        sums[which, k * nh + h] = value

        def go(off):
            for turn in range(nh):
                if isinstance(off, int) and off == 0 and turn == 0:
                    continue
                flat = off * nh + turn
                pltpu.make_async_remote_copy(
                    src_ref=sbuf.at[which], dst_ref=sums.at[which, k * nh + h], send_sem=s_send.at[which, flat],
                    recv_sem=s_recv.at[which, flat],
                    device_id=dev(lax.rem(k + off, ns), base + lax.rem(h + turn, nh)), device_id_type=MESH).start()

        go(0)
        each(1, ns, go)

    def sum_wait(which, turn):
        if turn != 0:
            sum_desc(which, 0, turn).wait_recv()
        each(1, ns, lambda off: sum_desc(which, off, turn).wait_recv())

    def total(which, j):
        return lax.fori_loop(
            0, ns, lambda i, acc: acc + sums[which, i * nh + j], jnp.zeros((1, LANES), F32))

    sum_send(0, jnp.sum(d * image, axis=0, keepdims=True))
    arrived(RES)
    hand_on(JAC)
    arrived(JAC)
    r = rfull[...]
    smooth = jacobi(jnp.concatenate([r, image], axis=1))
    jr, jim = smooth[:, :LANES], smooth[:, LANES:]
    send_face(1, pick(sel, jr))
    send_face(2, pick(sel, jim))

    hand_on(INV)
    arrived(INV)
    ih[:B, :], il[:B, :] = split(invf[...])
    ih[B:, :] = dot(sel, ih[:B, :]).astype(BF)
    il[B:, :] = dot(sel, il[:B, :]).astype(BF)

    rho = rho_ref[0:1, half]
    sum_wait(0, 0)
    alpha = rho / total(0, h)
    rn = r - alpha * image

    def rows_copy(which, turn):
        to = base + lax.rem(h + turn, nh)
        return pltpu.make_async_remote_copy(
            src_ref=rows_out.at[which, pl.ds(pl.multiple_of(to * gb, 8), gb), :], dst_ref=rows_in.at[which, turn],
            send_sem=r_send.at[which, turn], recv_sem=r_recv.at[which, turn], device_id=dev(k, to),
            device_id_type=MESH)

    rows_out[0] = rn
    for turn in range(1, nh):
        rows_copy(0, turn).start()
    wait_face(1)
    wait_face(2)
    s = jr - alpha * jim
    faces = jnp.concatenate(
        [s] + [face_in[1, side] - alpha * face_in[2, side] for side in range(2)], axis=0)
    defect = rn - mm(mh[...], ml[...], faces)
    both = mm(ih[...], il[...], defect)
    solved = both[:B, :]
    tu[2, k] = both[B:, :]
    each(1, ns, lambda off: tu_copy(2, off).start())

    for which in range(2):
        each(1, ns, functools.partial(tu_hand_on, which))
    def nearest(i):
        step = i // 2
        return 1 + step + (i % 2) * (ns - 2 - 2 * step)

    each(0, ns - 1, lambda i: tu_hand_on(2, nearest(i)))
    for which in range(3):
        for turn in range(1, passes[which]):
            each(1, ns, lambda off: tu_pass(which, turn, off).wait_recv())

    def forward(i, prev):
        fps[i] = prev
        return tu[2, i] + mm(*split(tu[0, i]), prev)

    last = lax.fori_loop(0, ns, forward, jnp.zeros((IF, LANES), F32), unroll=ns <= 8)
    fps[ns] = last

    def backward(t, nxt):
        i = ns - 1 - t
        offs[i] = nxt
        return fps[i + 1] + mm(*split(tu[1, i]), nxt)

    lax.fori_loop(0, ns, backward, jnp.zeros((IF, LANES), F32), unroll=ns <= 8)
    ends = jnp.concatenate([fps[k], offs[k]], axis=0)
    precond = s + (solved - mm(*split(fback[...]), ends))
    rows_out[1] = precond
    for turn in range(1, nh):
        rows_copy(1, turn).start()
    sum_send(1, jnp.sum(rn * precond, axis=0, keepdims=True))

    def put(j_half, alpha_j, res_rows, turn):
        cols = pl.ds(pl.multiple_of(j_half * LANES, LANES), LANES)
        out_it[:, cols] = it_ref[:, cols] + alpha_j * dir_ref[:, cols]
        out_res[:, cols] = res_rows

    put(h, alpha, rows_out[0, mine, :], 0)
    for turn in range(1, nh):
        sum_wait(0, turn)
        j = lax.rem(h + nh - turn, nh)
        rows_copy(0, turn).wait_recv()
        cols = pl.ds(pl.multiple_of(j * LANES, LANES), LANES)
        put(j, rho_ref[0:1, cols] / total(0, j), rows_in[0, turn], turn)

    for turn in range(nh):
        sum_wait(1, turn)
        j = lax.rem(h + nh - turn, nh)
        cols = pl.ds(pl.multiple_of(j * LANES, LANES), LANES)
        new = total(1, j)
        out_rho[0:1, cols] = new
        if turn:
            rows_copy(1, turn).wait_recv()
            part = rows_in[1, turn]
        else:
            part = rows_out[1, mine, :]
        out_dir[:, cols] = part + new / rho_ref[0:1, cols] * dir_ref[:, cols]

    for m in range(len(mats)):
        for off in range(1, ng):
            mat_copy(m, off).wait_send()
    for slot in range(3):
        @pl.when(k < ns - 1)
        def _():
            face_copy(slot, 0).wait_send()

        @pl.when(k > 0)
        def _():
            face_copy(slot, 1).wait_send()
    for which in range(3):
        each(1, ns, lambda off: tu_copy(which, off).wait_send())
        for turn in range(1, passes[which]):
            each(1, ns, lambda off: tu_pass(which, turn, off).wait_send())
    for which in range(2):
        for turn in range(1, nh):
            rows_copy(which, turn).wait_send()
            sum_desc(which, 0, turn).wait_send()
        for turn in range(nh):
            each(1, ns, lambda off: sum_desc(which, off, turn).wait_send())


def local(ns, ng, iterate, residual, direction, prior_rho, *rest):
    gb, cols = direction.shape
    nh = cols // LANES
    B = gb * ng
    IF = rest[1].shape[1]
    row = jax.ShapeDtypeStruct((gb, cols), F32)
    V = pltpu.VMEM
    DMA = pltpu.SemaphoreType.DMA
    vm = pl.BlockSpec(memory_space=pltpu.VMEM)
    out = pl.pallas_call(
        functools.partial(kernel, ns, ng, nh),
        out_shape=(row, row, row, jax.ShapeDtypeStruct((1, cols), F32)),
        in_specs=[vm if i in (3, 7) else pl.BlockSpec(memory_space=pl.ANY) for i in range(12)],
        out_specs=(vm,) * 4,
        scratch_shapes=[
            V((B, LANES), F32), V((B, LANES), F32), V((B, B), F32), V((B, IF), F32), V((B, IF), F32),
            V((B, gb), F32), V((B, B), F32), V((B, IF), F32), V((B, IF), F32),
            V((B, B + 2 * IF), BF), V((B, B + 2 * IF), BF), V((B + IF, B), BF), V((B + IF, B), BF),
            V((3, IF, LANES), F32), V((3, 2, IF, LANES), F32), V((3, ns, IF, LANES), F32),
            V((ns, IF, LANES), F32), V((ns + 1, IF, LANES), F32), V((B, 2 * IF), F32), V((gb, IF), F32), V((B, IF), F32),
            *[V(a.shape, F32) for a in (iterate, residual, direction, *rest[:1], *rest[1:3], *rest[4:])], DMA((10,)),
            V((2, 1, LANES), F32), V((2, ns * nh, 1, LANES), F32),
            V((2, B, LANES), F32), V((2, nh, gb, LANES), F32),
            DMA((10, ng)), DMA((10, ng)), DMA((3, 2)), DMA((3, 2)), DMA((3, ns)), DMA((3, ns)),
            DMA((2, ns * nh)), DMA((2, ns * nh)), DMA((2, nh)), DMA((2, nh)), DMA((3, max(nh, ng // nh), ns)), DMA((3, max(nh, ng // nh), ns)),
        ],
        compiler_params=pltpu.CompilerParams(
            collective_id=0, has_side_effects=True, vmem_limit_bytes=60 * 1024 * 1024),
    )(iterate, residual, direction, prior_rho.reshape(1, cols), *rest)
    return out[0], out[1], out[2], out[3].reshape(cols)


def solution(mesh):
    rows = P(("slab", "grp"), None)
    in_specs = (rows, rows, rows, P(), rows, rows, rows, P("slab", None), rows, rows, rows, rows)
    out_specs = (rows, rows, rows, P())
    body = functools.partial(local, mesh.shape["slab"], mesh.shape["grp"])
    return jax.shard_map(body, mesh=mesh, in_specs=in_specs, out_specs=out_specs, check_vma=False)
```
